32 devices in a mesh: gx: 2 (over x), gy: 4 (over y, core), gz: 4 (over z).
Axes of the slice: x: 2, y: 2, z: 4, core: 2. Of those that a mesh axis runs over, the one named last changes fastest.
Arguments:
- node_feat: bfloat16 [16, 32, 32, 128], P('gx', 'gy', 'gz'), may hold values from -6 to 6
- edge_feat: bfloat16 [4, 16, 32, 32, 128], P(None, 'gx', 'gy', 'gz'), may hold values from -6 to 6
- copies: int32 [16, 32, 32], P('gx', 'gy', 'gz'), may hold values from 1 to 8
- offsets: int32 [4, 3], replicated, may hold values from -1 to 1
- w_edge_in: bfloat16 [384, 128], replicated, may hold values from -0.3125 to 0.3125
- w_edge_out: bfloat16 [128, 128], replicated, may hold values from -0.5 to 0.5
- w_node_in: bfloat16 [256, 128], replicated, may hold values from -0.375 to 0.375
- w_node_out: bfloat16 [128, 128], replicated, may hold values from -0.5 to 0.5
- node_cot: bfloat16 [16, 32, 32, 128], P('gx', 'gy', 'gz'), may hold values from -6 to 6
Outputs:
- node_grad: bfloat16 [16, 32, 32, 128], P('gx', 'gy', 'gz')
- edge_grad: bfloat16 [4, 16, 32, 32, 128], P(None, 'gx', 'gy', 'gz')
- grad_edge_in: float32 [384, 128], replicated
- grad_edge_out: float32 [128, 128], replicated
- grad_node_in: float32 [256, 128], replicated
- grad_node_out: float32 [128, 128], replicated
The draws below stay inside these ranges and needn't reach their ends.
Inputs may be any that keep to these rules, and one draw needn't show every extreme that they name: `offsets`: each row is one lattice offset, its three entries along the first, second and third dimension.
All inputs are finite; a program needn't handle non-finite values.
Results may differ from the reference program's by a relative error of at most 0.0068.
Values sent between devices are 32-bit elements; how exact they have to be, the bound alone decides.
A program may use at most 64 MiB of HBM per device.

```python
import math
import jax
import jax.numpy as jnp
from jax import lax

WIDTH = 128
KINDS = 4
BRICK = 8
NX = 16
NY = 32
NZ = 32
N_GX = 2
N_GY = 4
N_GZ = 4


def place_ends(values, rng, low, high):
    longest = values.shape.index(max(values.shape))
    spots = []
    for shift in (0, 1):
        where = [jax.random.randint(jax.random.fold_in(rng, axis), (), 0, length) for axis, length in enumerate(values.shape)]
        where[longest] = (where[longest] + shift) % values.shape[longest]
        spots.append(tuple(where))
    return values.at[spots[0]].set(low).at[spots[1]].set(high)


def block_levels(own_key, extent, shards, least, top_value):
    level, own = 1.0, jax.random.fold_in(own_key, 6)
    for dim, blocks in shards:
        heights = jnp.exp(jax.random.uniform(jax.random.fold_in(own, dim), (blocks,), jnp.float32, least / len(shards), top_value / len(shards)))
        level = level * jnp.repeat(heights, extent[dim] // blocks).reshape([-1 if axis == dim else 1 for axis in range(len(extent))])
    return level


def bell_draw(rng, dims, scale, most, cuts=(), held_as=jnp.bfloat16):
    values = jax.random.normal(rng, dims, jnp.float32) * scale
    if len(cuts) > 0:
        values = block_levels(rng, dims, cuts, -0.22, 0.18) * values
    return jnp.clip(values, min=-most, max=most).astype(held_as)


def setup_inputs(seed: int = 0) -> dict:
    keys = jax.random.split(jax.random.key(seed), 10)
    node_feat = bell_draw(keys[0], (NX, NY, NZ, WIDTH), 1.0, 6.0, ((0, 2), (1, 4), (2, 4)))
    edge_feat = bell_draw(keys[1], (KINDS, NX, NY, NZ, WIDTH), 1.0, 6.0, ((1, 2), (2, 4), (3, 4)))
    copies = place_ends(jax.random.randint(keys[2], (NX, NY, NZ), 1, 9), jax.random.fold_in(keys[2], 1), 1, 8).astype(jnp.int32)
    offsets = place_ends(jax.random.randint(keys[3], (KINDS, 3), -1, 2), jax.random.fold_in(keys[3], 1), -1, 1).astype(jnp.int32)
    w_edge_in = bell_draw(keys[4], (3 * WIDTH, WIDTH), (3 * WIDTH) ** -0.5, 0.3125)
    w_edge_out = bell_draw(keys[5], (WIDTH, WIDTH), WIDTH ** -0.5, 0.5)
    w_node_in = bell_draw(keys[6], (2 * WIDTH, WIDTH), (2 * WIDTH) ** -0.5, 0.375)
    w_node_out = bell_draw(keys[7], (WIDTH, WIDTH), WIDTH ** -0.5, 0.5)
    node_cot = bell_draw(keys[8], (NX, NY, NZ, WIDTH), 1.0, 6.0, ((0, 2), (1, 4), (2, 4)))
    return dict(node_feat=node_feat, edge_feat=edge_feat, copies=copies, offsets=offsets, w_edge_in=w_edge_in, w_edge_out=w_edge_out, w_node_in=w_node_in, w_node_out=w_node_out, node_cot=node_cot)


def neighbour_valid(offset, brick):
    coords = jnp.arange(brick, dtype=jnp.int32)
    inside = [(coords + offset[which] >= 0) & (coords + offset[which] < brick) for which in range(3)]
    joined = inside[0][:, None, None] & inside[1][None, :, None] & inside[2][None, None, :]
    return joined.astype(jnp.float32).reshape(brick * brick * brick, 1)

def moved_view(field, corner):
    padded = jnp.pad(field, ((1, 1), (1, 1), (1, 1), (0, 0)))
    start = (1 + corner).astype(jnp.int32)
    return lax.dynamic_slice(padded, (start[0], start[1], start[2], jnp.int32(0)), field.shape)

def silu_slope(preact):
    sigma = jax.nn.sigmoid(preact)
    return sigma * (1.0 + preact * (1.0 - sigma))

def outer_product(left, right):
    return lax.dot_general(left, right, (((0,), (0,)), ((), ())), preferred_element_type=jnp.float32)

def edge_preact(sender, receiver, feature, w_edge_in, width):
    total = jnp.dot(sender, w_edge_in[:width], preferred_element_type=jnp.float32)
    total = total + jnp.dot(receiver, w_edge_in[width:2 * width], preferred_element_type=jnp.float32)
    return total + jnp.dot(feature, w_edge_in[2 * width:], preferred_element_type=jnp.float32)

def edge_messages(nodes, edges, offsets, w_edge_in, w_edge_out):
    brick = nodes.shape[0]
    width = nodes.shape[3]
    count = brick * brick * brick
    receiver = nodes.reshape(count, width)
    total = jnp.zeros((count, width), jnp.float32)
    preacts = []
    hiddens = []
    for kind_index in range(edges.shape[0]):
        offset = offsets[kind_index]
        sender = moved_view(nodes, offset).reshape(count, width)
        preact = edge_preact(sender, receiver, edges[kind_index].reshape(count, width), w_edge_in, width)
        hidden = jax.nn.silu(preact).astype(jnp.bfloat16)
        message = jnp.dot(hidden, w_edge_out, preferred_element_type=jnp.float32)
        total = total + neighbour_valid(offset, brick) * message
        preacts.append(preact)
        hiddens.append(hidden)
    return (total.reshape(nodes.shape), jnp.stack(preacts), jnp.stack(hiddens))

def node_backward(nodes, summed, copies, node_cot, w_node_in, w_node_out):
    width = nodes.shape[3]
    count = nodes.shape[0] * nodes.shape[1] * nodes.shape[2]
    receiver = nodes.reshape(count, width)
    scale = copies.reshape(count, 1).astype(jnp.float32)
    gathered = (summed.reshape(count, width) / scale).astype(jnp.bfloat16)
    preact = jnp.dot(receiver, w_node_in[:width], preferred_element_type=jnp.float32)
    preact = preact + jnp.dot(gathered, w_node_in[width:], preferred_element_type=jnp.float32)
    hidden = jax.nn.silu(preact).astype(jnp.bfloat16)
    upstream = node_cot.reshape(count, width)
    grad_out = outer_product(hidden, upstream)
    slope = (jnp.dot(upstream, w_node_out.T, preferred_element_type=jnp.float32) * silu_slope(preact)).astype(jnp.bfloat16)
    grad_in = jnp.concatenate([outer_product(receiver, slope), outer_product(gathered, slope)], axis=0)
    to_nodes = jnp.dot(slope, w_node_in[:width].T, preferred_element_type=jnp.float32)
    to_agg = jnp.dot(slope, w_node_in[width:].T, preferred_element_type=jnp.float32) / scale
    return (to_nodes.reshape(nodes.shape), to_agg.reshape(nodes.shape), grad_in, grad_out)

def edge_backward(nodes, edges, offsets, incoming, w_edge_in, w_edge_out, preacts, hiddens):
    brick = nodes.shape[0]
    width = nodes.shape[3]
    count = brick * brick * brick
    receiver = nodes.reshape(count, width)
    arriving = incoming.reshape(count, width)
    grad_in = jnp.zeros((3 * width, width), jnp.float32)
    grad_out = jnp.zeros((width, width), jnp.float32)
    to_nodes = jnp.zeros((count, width), jnp.float32)
    sent_back = jnp.zeros(nodes.shape, jnp.float32)
    edge_grads = []
    for kind_index in range(edges.shape[0]):
        offset = offsets[kind_index]
        sender = moved_view(nodes, offset).reshape(count, width)
        feature = edges[kind_index].reshape(count, width)
        message_cot = (neighbour_valid(offset, brick) * arriving).astype(jnp.bfloat16)
        grad_out = grad_out + outer_product(hiddens[kind_index], message_cot)
        slope = jnp.dot(message_cot, w_edge_out.T, preferred_element_type=jnp.float32) * silu_slope(preacts[kind_index])
        slope = slope.astype(jnp.bfloat16)
        grad_in = grad_in + jnp.concatenate([outer_product(sender, slope), outer_product(receiver, slope), outer_product(feature, slope)], axis=0)
        to_nodes = to_nodes + jnp.dot(slope, w_edge_in[width:2 * width].T, preferred_element_type=jnp.float32)
        from_sender = jnp.dot(slope, w_edge_in[:width].T, preferred_element_type=jnp.float32).reshape(nodes.shape)
        sent_back = sent_back + moved_view(from_sender, -offset)
        edge_grads.append(jnp.dot(slope, w_edge_in[2 * width:].T, preferred_element_type=jnp.float32).astype(jnp.bfloat16).reshape(nodes.shape))
    return (to_nodes.reshape(nodes.shape) + sent_back, jnp.stack(edge_grads), grad_in, grad_out)

def clip_all(grads):
    squares = sum((jnp.sum(single * single) for single in grads))
    entries = sum((single.size for single in grads))
    factor = math.sqrt(entries) / jnp.sqrt(squares)
    return tuple((single * factor for single in grads))

def to_bricks(array):
    rest = array.shape[3:]
    shaped = array.reshape((N_GX, BRICK, N_GY, BRICK, N_GZ, BRICK) + rest)
    order = (0, 2, 4, 1, 3, 5) + tuple(range(6, 6 + len(rest)))
    return jnp.transpose(shaped, order).reshape((N_GX * N_GY * N_GZ, BRICK, BRICK, BRICK) + rest)

def from_bricks(array):
    rest = array.shape[4:]
    shaped = array.reshape((N_GX, N_GY, N_GZ, BRICK, BRICK, BRICK) + rest)
    order = (0, 3, 1, 4, 2, 5) + tuple(range(6, 6 + len(rest)))
    return jnp.transpose(shaped, order).reshape((N_GX * BRICK, N_GY * BRICK, N_GZ * BRICK) + rest)

def shift_blocks(block, brick_axis, forward):
    length = block.shape[brick_axis]
    empty = jnp.zeros_like(lax.slice_in_dim(block, 0, 1, axis=brick_axis))
    if forward:
        return jnp.concatenate([empty, lax.slice_in_dim(block, 0, length - 1, axis=brick_axis)], axis=brick_axis)
    return jnp.concatenate([lax.slice_in_dim(block, 1, length, axis=brick_axis), empty], axis=brick_axis)

def assemble_all(stacked):
    grid = stacked.reshape((N_GX, N_GY, N_GZ, BRICK, BRICK, BRICK) + stacked.shape[4:])
    for brick_axis in range(3):
        local_axis = brick_axis + 3
        lower = lax.slice_in_dim(grid, 0, 1, axis=local_axis)
        upper = lax.slice_in_dim(grid, BRICK - 1, BRICK, axis=local_axis)
        middle = lax.slice_in_dim(grid, 1, BRICK - 1, axis=local_axis)
        new_lower = lower + shift_blocks(upper, brick_axis, True)
        new_upper = upper + shift_blocks(lower, brick_axis, False)
        grid = jnp.concatenate([new_lower, middle, new_upper], axis=local_axis)
    return grid.reshape(stacked.shape)

def reference(node_feat, edge_feat, copies, offsets, w_edge_in, w_edge_out, w_node_in, w_node_out, node_cot):
    width = node_feat.shape[3]
    nodes_b = to_bricks(node_feat)
    edges_b = jnp.moveaxis(to_bricks(jnp.moveaxis(edge_feat, 0, 3)), 4, 1)
    copies_b = to_bricks(copies)
    cot_b = to_bricks(node_cot)

    def forward_one(items):
        return edge_messages(items[0], items[1], offsets, w_edge_in, w_edge_out)[0]
    local_sum = lax.map(forward_one, (nodes_b, edges_b))
    summed = assemble_all(local_sum)

    def node_step(carry, items):
        to_nodes, to_agg, grad_in, grad_out = node_backward(items[0], items[1], items[2], items[3], w_node_in, w_node_out)
        return ((carry[0] + grad_in, carry[1] + grad_out), (to_nodes, to_agg))
    start_node = (jnp.zeros((2 * width, width), jnp.float32), jnp.zeros((width, width), jnp.float32))
    node_grads, node_outputs = lax.scan(node_step, start_node, (nodes_b, summed, copies_b, cot_b))
    node_part, agg_part = node_outputs
    incoming = assemble_all(agg_part)

    def edge_step(carry, items):
        nodes, edges, arriving = items
        unused, preacts, hiddens = edge_messages(nodes, edges, offsets, w_edge_in, w_edge_out)
        to_nodes, edge_grads, grad_in, grad_out = edge_backward(nodes, edges, offsets, arriving, w_edge_in, w_edge_out, preacts, hiddens)
        return ((carry[0] + grad_in, carry[1] + grad_out), (to_nodes, edge_grads))
    start_edge = (jnp.zeros((3 * width, width), jnp.float32), jnp.zeros((width, width), jnp.float32))
    edge_grads_w, edge_outputs = lax.scan(edge_step, start_edge, (nodes_b, edges_b, incoming))
    edge_part, edge_grad_b = edge_outputs
    local = cot_b.astype(jnp.float32) + node_part + edge_part
    node_grad = from_bricks(assemble_all(local)).astype(jnp.bfloat16)
    edge_grad = jnp.moveaxis(from_bricks(jnp.moveaxis(edge_grad_b, 1, 4)), 3, 0)
    clipped = clip_all((edge_grads_w[0], edge_grads_w[1], node_grads[0], node_grads[1]))
    return (node_grad, edge_grad, clipped[0], clipped[1], clipped[2], clipped[3])
```

```python
import functools
import math

import jax
import jax.numpy as jnp
from jax import lax
from jax.experimental import pallas as pl
from jax.experimental.pallas import tpu as pltpu
from jax.sharding import PartitionSpec as P

F32 = jnp.float32
BF16 = jnp.bfloat16
AXES = ("gx", "gy", "gz")
DIRS = [
    (dx, dy, dz)
    for dx in (-1, 0, 1)
    for dy in (-1, 0, 1)
    for dz in (-1, 0, 1)
    if (dx, dy, dz) != (0, 0, 0)
]


def dot(left, right):
    return jnp.dot(left, right, preferred_element_type=F32)


def dot_t(left, right):
    return lax.dot_general(left, right, (((1,), (1,)), ((), ())), preferred_element_type=F32)


def outer(left, right):
    return lax.dot_general(left, right, (((0,), (0,)), ((), ())), preferred_element_type=F32)


def class_slot(d):
    slot = 0
    for step in d:
        if step != 0:
            slot = slot * 2 + (0 if step < 0 else 1)
    return "".join("xyz"[i] for i in range(3) if d[i] != 0), slot


def part(ref, lead, d, edge, low):
    where = list(lead)
    for step in d[:2]:
        if step == 0:
            where.append(slice(None))
        else:
            where.append(edge if (step > 0) != low else 0)
    return ref.at[tuple(where)]


def kernel(
    sizes, group, rest,
    offs, node_ref, edge_ref, cop_ref, wei, weo, wni, wno, cot_ref,
    o_node, o_edge, o_ei, o_eo, o_ni, o_no,
    edges, egr, pad_a, pad_s, sl, hs, field, zs, field2,
    rx, ry, rz, rxy, rxz, ryz, rxyz,
    ng, eg, gn, ge, rbn, rbe, exn, exe,
    in_sem, out_sem, hs_sem, hr_sem, rs_s, rs_r, ex_s, ex_r, ag_s, ag_r,
):
    width = node_ref.shape[1]
    count = node_ref.shape[0]
    brick = field.shape[1]
    kinds = offs.shape[0]
    edge = brick - 1
    cube = (brick, brick, brick, width)
    pos = {a: lax.axis_index(a) for a in AXES}
    recv = {"x": rx, "y": ry, "z": rz, "xy": rxy, "xz": rxz, "yz": ryz, "xyz": rxyz}

    fetch = pltpu.make_async_copy(edge_ref, edges, in_sem)
    fetch.start()

    def exists(d, sign):
        ok = None
        for a, step in zip(AXES, d):
            if step != 0:
                here = pos[a] + sign * step
                one = (here >= 0) & (here < sizes[a])
                ok = one if ok is None else ok & one
        return ok

    def shifted(d, sign):
        return {a: pos[a] + sign * step for a, step in zip(AXES, d)}

    def rank_of(axes):
        rank = 0
        for a in axes:
            rank = rank * sizes[a] + pos[a]
        return rank

    def place_of(axes, rank):
        place = dict(pos)
        for a in reversed(axes):
            place[a] = lax.rem(rank, sizes[a])
            rank = rank // sizes[a]
        return place

    members = math.prod(sizes[a] for a in group)
    me = rank_of(group)

    barrier = pltpu.get_barrier_semaphore()

    def greet(place):
        pl.semaphore_signal(
            barrier, inc=1, device_id=place, device_id_type=pl.DeviceIdType.MESH
        )

    waits = jnp.int32(members - 1 + sum(sizes[a] - 1 for a in rest))
    for j in range(1, members):
        greet(place_of(group, lax.rem(me + j, members)))
    for a in rest:
        for j in range(1, sizes[a]):
            greet(place_of((a,), lax.rem(pos[a] + j, sizes[a])))
    for d in DIRS:
        ok = exists(d, 1)
        waits = waits + ok.astype(jnp.int32)

        @pl.when(ok)
        def _(d=d):
            greet(shifted(d, 1))

    def halo_copy(a, i, d, place):
        name, slot = class_slot(d)
        if d[2] == 0:
            src = part(field, (a,), d, edge, False)
        else:
            src = part(zs, (a, 0 if d[2] < 0 else 1), d, edge, False)
        return pltpu.make_async_remote_copy(
            src_ref=src,
            dst_ref=recv[name].at[a, slot],
            send_sem=hs_sem.at[a, i],
            recv_sem=hr_sem.at[a, i],
            device_id=place,
            device_id_type=pl.DeviceIdType.MESH,
        )

    def halo_start(a, values):
        values = values.reshape(cube)
        field[a] = values
        zs[a, 0] = values[:, :, 0:1, :]
        zs[a, 1] = values[:, :, edge:, :]
        for i, d in enumerate(DIRS):

            @pl.when(exists(d, 1))
            def _(i=i, d=d):
                halo_copy(a, i, d, shifted(d, 1)).start()

        field2[a] = values

    def halo_finish(a):
        for i, d in enumerate(DIRS):

            @pl.when(exists(d, -1))
            def _(i=i, d=d):
                halo_copy(a, i, d, shifted(d, -1)).wait_recv()
                name, slot = class_slot(d)
                where = [a]
                for step in d[:2]:
                    where.append(slice(None) if step == 0 else (0 if step > 0 else edge))
                if d[2] != 0:
                    where.append(slice(0, 1) if d[2] > 0 else slice(edge, brick))
                where = tuple(where)
                field2[where] = field2[where] + recv[name][a, slot]

        return field2[a].reshape(count, width)

    def halo_drain(a):
        for i, d in enumerate(DIRS):

            @pl.when(exists(d, 1))
            def _(i=i, d=d):
                halo_copy(a, i, d, shifted(d, 1)).wait_send()

    def rows_at(ref, rank, rows):
        return ref.at[pl.ds(pl.multiple_of(rank * rows, 8), rows)]

    def rs_copy(w, j):
        src, dst = (ng, rbn) if w == 0 else (eg, rbe)
        to = lax.rem(me + j, members)
        rows = src.shape[0] // members
        return pltpu.make_async_remote_copy(
            src_ref=rows_at(src, to, rows),
            dst_ref=dst.at[j],
            send_sem=rs_s.at[w, j],
            recv_sem=rs_r.at[w, j],
            device_id=place_of(group, to),
            device_id_type=pl.DeviceIdType.MESH,
        )

    def rs_start(w):
        for j in range(1, members):
            rs_copy(w, j).start()

    def rs_finish(w):
        src, dst = (ng, rbn) if w == 0 else (eg, rbe)
        rows = src.shape[0] // members
        total = rows_at(src, me, rows)[...]
        for j in range(1, members):
            rs_copy(w, j).wait_recv()
            total = total + dst[j]
        return total

    bases = []
    base = 0
    for a in rest:
        bases.append(base)
        base += sizes[a]

    def ex_copy(w, e, j):
        buf = exn if w == 0 else exe
        a = rest[e]
        spot = buf.at[bases[e] + pos[a]]
        return pltpu.make_async_remote_copy(
            src_ref=spot,
            dst_ref=spot,
            send_sem=ex_s.at[w, bases[e] + j],
            recv_sem=ex_r.at[w, bases[e] + j],
            device_id=place_of((a,), lax.rem(pos[a] + j, sizes[a])),
            device_id_type=pl.DeviceIdType.MESH,
        )

    def ex_start(w, e, total):
        buf = exn if w == 0 else exe
        buf[bases[e] + pos[rest[e]]] = total
        for j in range(1, sizes[rest[e]]):
            ex_copy(w, e, j).start()

    def ex_finish(w, e):
        buf = exn if w == 0 else exe
        for j in range(1, sizes[rest[e]]):
            ex_copy(w, e, j).wait_recv()
        total = buf[bases[e]]
        for r in range(1, sizes[rest[e]]):
            total = total + buf[bases[e] + r]
        return total

    def ex_all(w):
        for e in range(len(rest)):
            total = ex_finish(w, e)
            if e + 1 < len(rest):
                ex_start(w, e + 1, total)
        return total

    def ag_copy(w, j):
        buf = gn if w == 0 else ge
        spot = rows_at(buf, me, buf.shape[0] // members)
        return pltpu.make_async_remote_copy(
            src_ref=spot,
            dst_ref=spot,
            send_sem=ag_s.at[w, j],
            recv_sem=ag_r.at[w, j],
            device_id=place_of(group, lax.rem(me + j, members)),
            device_id_type=pl.DeviceIdType.MESH,
        )

    def ag_start(w, total):
        buf = gn if w == 0 else ge
        rows_at(buf, me, buf.shape[0] // members)[...] = total
        for j in range(1, members):
            ag_copy(w, j).start()

    def ag_finish(w):
        for j in range(1, members):
            ag_copy(w, j).wait_recv()

    node = node_ref[...]
    pad_a[...] = jnp.zeros_like(pad_a)
    pad_s[...] = jnp.zeros_like(pad_s)
    pad_a[1 : brick + 1, 1 : brick + 1] = dot(node, wei[:width]).reshape(cube)
    received = dot(node, wei[width : 2 * width])
    coords = [lax.broadcasted_iota(jnp.int32, cube, axis) for axis in range(3)]
    scale_rows = lax.broadcasted_iota(jnp.int32, (count, brick * brick), 0) // brick
    scale_cols = lax.broadcasted_iota(jnp.int32, (count, brick * brick), 1)
    picked = dot(
        (scale_rows == scale_cols).astype(BF16), cop_ref[...].astype(F32).astype(BF16)
    )
    lane = lax.broadcasted_iota(jnp.int32, (count, brick), 1)
    row = lax.broadcasted_iota(jnp.int32, (count, brick), 0) % brick
    picked = jnp.where(lane == row, picked, 0.0).astype(BF16)
    inverse = 1.0 / dot(picked, jnp.ones((brick, width), BF16))
    fetch.wait()
    hiddens = []
    hidden_sum = None
    for k in range(kinds):
        o = [offs[k, axis] for axis in range(3)]
        sent = pad_a[pl.ds(1 + o[0], brick), pl.ds(1 + o[1], brick)]
        sent = pltpu.roll(sent.reshape(brick * brick, brick, width), lax.rem(brick - o[2], brick), 1)
        pre = dot(edges[k * count : (k + 1) * count], wei[2 * width :])
        pre = pre + received + sent.reshape(count, width)
        sigma = 0.5 * jnp.tanh(0.5 * pre) + 0.5
        hidden = pre * sigma
        valid = None
        for axis in range(3):
            here = coords[axis] + o[axis]
            one = (here >= 0) & (here < brick)
            valid = one if valid is None else valid & one
        valid = valid.reshape(count, width)
        sl[k] = jnp.where(valid, sigma + hidden * (1.0 - sigma), 0.0)
        hidden = jnp.where(valid, hidden, 0.0).astype(BF16)
        hiddens.append(hidden)
        wide = hidden.astype(F32)
        hidden_sum = wide if hidden_sum is None else hidden_sum + wide
    w_out = weo[...]
    local_sum = dot(
        jnp.concatenate(hiddens, axis=1), jnp.concatenate([w_out] * kinds, axis=0)
    )
    pl.semaphore_wait(barrier, waits)
    halo_start(0, local_sum)

    hs[...] = hidden_sum.astype(BF16)
    cot = cot_ref[...]
    node_own = dot(node, wni[:width])
    upstream = dot_t(cot, wno[...])

    summed = halo_finish(0)
    gathered = (summed * inverse).astype(BF16)
    pre = node_own + dot(gathered, wni[width:])
    sigma = 0.5 * jnp.tanh(0.5 * pre) + 0.5
    hidden = pre * sigma
    slope = (upstream * (sigma + hidden * (1.0 - sigma))).astype(BF16)
    halo_start(1, dot_t(slope, wni[width:]) * inverse)
    ng[:width] = outer(node, slope)
    ng[width : 2 * width] = outer(gathered, slope)
    ng[2 * width :] = outer(hidden.astype(BF16), cot)
    rs_start(0)
    own = cot.astype(F32) + dot_t(slope, wni[:width])

    arriving = halo_finish(1).astype(BF16)
    back = dot_t(arriving, w_out)
    slopes = []
    direct = None
    turned = None
    for k in range(kinds):
        o = [offs[k, axis] for axis in range(3)]
        slope = (back * sl[k]).astype(BF16)
        slopes.append(slope)
        wide = slope.astype(F32)
        direct = wide if direct is None else direct + wide
        pad_s[k, 1 : brick + 1, 1 : brick + 1] = wide.reshape(cube)
        moved = pad_s[k, pl.ds(1 - o[0], brick), pl.ds(1 - o[1], brick)]
        moved = pltpu.roll(moved.reshape(brick * brick, brick, width), lax.rem(brick + o[2], brick), 1)
        turned = moved if turned is None else turned + moved
    turned = turned.reshape(count, width).astype(BF16)
    direct = direct.astype(BF16)
    slope_all = jnp.concatenate(slopes, axis=0)
    eg[:width] = outer(node, turned)
    eg[width : 2 * width] = outer(node, direct)
    eg[2 * width : 3 * width] = outer(edges[...], slope_all)
    eg[3 * width :] = outer(hs[...], arriving)
    rs_start(1)
    own = own + dot_t(turned, wei[:width]) + dot_t(direct, wei[width : 2 * width])
    halo_start(2, own)
    ex_start(0, 0, rs_finish(0))
    egr[...] = dot_t(slope_all, wei[2 * width :]).astype(BF16)
    store = pltpu.make_async_copy(egr, o_edge, out_sem)
    store.start()
    ex_start(1, 0, rs_finish(1))
    ag_start(0, ex_all(0))
    o_node[...] = halo_finish(2).astype(BF16)
    ag_start(1, ex_all(1))
    ag_finish(0)
    node_total = gn[...]
    squares = jnp.sum(node_total * node_total, axis=0, keepdims=True)
    ag_finish(1)
    edge_total = ge[...]
    squares = squares + jnp.sum(edge_total * edge_total, axis=0, keepdims=True)
    squares = jnp.sum(squares, axis=1, keepdims=True)
    entries = (ge.shape[0] + gn.shape[0]) * width
    factor = math.sqrt(entries) / jnp.sqrt(squares)
    o_ei[...] = edge_total[: 3 * width] * factor
    o_eo[...] = edge_total[3 * width :] * factor
    o_ni[...] = node_total[: 2 * width] * factor
    o_no[...] = node_total[2 * width :] * factor
    store.wait()
    for a in range(3):
        halo_drain(a)
    for w in range(2):
        for j in range(1, members):
            rs_copy(w, j).wait_send()
            ag_copy(w, j).wait_send()
        for e in range(len(rest)):
            for j in range(1, sizes[rest[e]]):
                ex_copy(w, e, j).wait_send()


def on_device(
    sizes, node_feat, edge_feat, copies, offsets, w_edge_in, w_edge_out, w_node_in, w_node_out, node_cot
):
    brick = node_feat.shape[0]
    width = node_feat.shape[3]
    kinds = edge_feat.shape[0]
    count = brick**3
    rows_n, rows_e = 3 * width, 4 * width
    group, rest = ("gx", "gy"), ("gz",)
    if math.gcd(rows_n, rows_e) % (8 * sizes["gx"] * sizes["gy"]) != 0:
        group, rest = ("gy",), ("gx", "gz")
    members = math.prod(sizes[a] for a in group)
    others = sum(sizes[a] for a in rest)
    vmem = pl.BlockSpec(memory_space=pltpu.VMEM)
    smem = pl.BlockSpec(memory_space=pltpu.SMEM)
    hbm = pl.BlockSpec(memory_space=pl.ANY)
    dma = pltpu.SemaphoreType.DMA
    b, w = brick, width
    outs = pl.pallas_call(
        functools.partial(kernel, sizes, group, rest),
        out_shape=(
            jax.ShapeDtypeStruct((count, w), BF16),
            jax.ShapeDtypeStruct((kinds * count, w), BF16),
            jax.ShapeDtypeStruct((3 * w, w), F32),
            jax.ShapeDtypeStruct((w, w), F32),
            jax.ShapeDtypeStruct((2 * w, w), F32),
            jax.ShapeDtypeStruct((w, w), F32),
        ),
        in_specs=[smem, vmem, hbm, vmem, vmem, vmem, vmem, vmem, vmem],
        out_specs=(vmem, hbm, vmem, vmem, vmem, vmem),
        scratch_shapes=[
            pltpu.VMEM((kinds * count, w), BF16),
            pltpu.VMEM((kinds * count, w), BF16),
            pltpu.VMEM((b + 2, b + 2, b, w), F32),
            pltpu.VMEM((kinds, b + 2, b + 2, b, w), F32),
            pltpu.VMEM((kinds, count, w), F32),
            pltpu.VMEM((count, w), BF16),
            pltpu.VMEM((3, b, b, b, w), F32),
            pltpu.VMEM((3, 2, b, b, 1, w), F32),
            pltpu.VMEM((3, b, b, b, w), F32),
            pltpu.VMEM((3, 2, b, b, w), F32),
            pltpu.VMEM((3, 2, b, b, w), F32),
            pltpu.VMEM((3, 2, b, b, 1, w), F32),
            pltpu.VMEM((3, 4, b, w), F32),
            pltpu.VMEM((3, 4, b, 1, w), F32),
            pltpu.VMEM((3, 4, b, 1, w), F32),
            pltpu.VMEM((3, 8, 1, w), F32),
            pltpu.VMEM((rows_n, w), F32),
            pltpu.VMEM((rows_e, w), F32),
            pltpu.VMEM((rows_n, w), F32),
            pltpu.VMEM((rows_e, w), F32),
            pltpu.VMEM((members, rows_n // members, w), F32),
            pltpu.VMEM((members, rows_e // members, w), F32),
            pltpu.VMEM((others, rows_n // members, w), F32),
            pltpu.VMEM((others, rows_e // members, w), F32),
            dma,
            dma,
            dma((3, len(DIRS))),
            dma((3, len(DIRS))),
            dma((2, members)),
            dma((2, members)),
            dma((2, others)),
            dma((2, others)),
            dma((2, members)),
            dma((2, members)),
        ],
        compiler_params=pltpu.CompilerParams(collective_id=0, has_side_effects=True),
    )(
        offsets,
        node_feat.reshape(count, w),
        edge_feat.reshape(kinds * count, w),
        copies.reshape(b * b, b),
        w_edge_in,
        w_edge_out,
        w_node_in,
        w_node_out,
        node_cot.reshape(count, w),
    )
    return (outs[0].reshape(node_feat.shape), outs[1].reshape(edge_feat.shape)) + tuple(outs[2:])


def solution(mesh):
    sizes = {a: mesh.shape[a] for a in AXES}
    bricks, edges = P("gx", "gy", "gz", None), P(None, "gx", "gy", "gz", None)
    return jax.shard_map(
        functools.partial(on_device, sizes),
        mesh=mesh,
        in_specs=(bricks, edges, P("gx", "gy", "gz"), P(), P(), P(), P(), P(), bricks),
        out_specs=(bricks, edges, P(), P(), P(), P()),
        check_vma=False,
    )
```

```python
import functools
import math

import jax
import jax.numpy as jnp
from jax import lax
from jax.experimental import pallas as pl
from jax.experimental.pallas import tpu as pltpu
from jax.sharding import PartitionSpec as P

F32 = jnp.float32
BF16 = jnp.bfloat16
VMEM_MAIN = 20 * 2**20
VMEM_FINISH = 8 * 2**20
FIN = pl.BlockSpec(memory_space=pl.ANY)
AXES = ("gx", "gy", "gz")
DIRS = [
    (dx, dy, dz)
    for dx in (-1, 0, 1)
    for dy in (-1, 0, 1)
    for dz in (-1, 0, 1)
    if (dx, dy, dz) != (0, 0, 0)
]


def dot(left, right):
    return jnp.dot(left, right, preferred_element_type=F32)


def dot_t(left, right):
    return lax.dot_general(left, right, (((1,), (1,)), ((), ())), preferred_element_type=F32)


def outer(left, right):
    return lax.dot_general(left, right, (((0,), (0,)), ((), ())), preferred_element_type=F32)


def class_slot(d):
    slot = 0
    for step in d:
        if step != 0:
            slot = slot * 2 + (0 if step < 0 else 1)
    return "".join("xyz"[i] for i in range(3) if d[i] != 0), slot


def part(ref, lead, d, edge, low):
    where = list(lead)
    for step in d[:2]:
        if step == 0:
            where.append(slice(None))
        else:
            where.append(edge if (step > 0) != low else 0)
    return ref.at[tuple(where)]


def kernel(
    sizes, group, rest,
    offs, node_ref, edge_ref, cop_ref, wei, weo, wni, wno, cot_ref,
    o_node, o_edge, gn, ga, gb,
    edges, egr, pad_a, pad_s, sl, field, zs, field2,
    rx, ry, rz, rxy, rxz, ryz, rxyz,
    ng, ea, eb, rbn, rba, rbb, exn, exa, exb,
    in_sem, out_sem, hs_sem, hr_sem, rs_s, rs_r, ex_s, ex_r, ag_s, ag_r,
):
    width = node_ref.shape[1]
    count = node_ref.shape[0]
    brick = field.shape[1]
    kinds = offs.shape[0]
    edge = brick - 1
    cube = (brick, brick, brick, width)
    pos = {a: lax.axis_index(a) for a in AXES}
    recv = {"x": rx, "y": ry, "z": rz, "xy": rxy, "xz": rxz, "yz": ryz, "xyz": rxyz}

    fetch = pltpu.make_async_copy(edge_ref, edges, in_sem)
    fetch.start()

    def exists(d, sign):
        ok = None
        for a, step in zip(AXES, d):
            if step != 0:
                here = pos[a] + sign * step
                one = (here >= 0) & (here < sizes[a])
                ok = one if ok is None else ok & one
        return ok

    def shifted(d, sign):
        return {a: pos[a] + sign * step for a, step in zip(AXES, d)}

    def rank_of(axes):
        rank = 0
        for a in axes:
            rank = rank * sizes[a] + pos[a]
        return rank

    def place_of(axes, rank):
        place = dict(pos)
        for a in reversed(axes):
            place[a] = lax.rem(rank, sizes[a])
            rank = rank // sizes[a]
        return place

    members = math.prod(sizes[a] for a in group)
    me = rank_of(group)

    barrier = pltpu.get_barrier_semaphore()

    def greet(place):
        pl.semaphore_signal(
            barrier, inc=1, device_id=place, device_id_type=pl.DeviceIdType.MESH
        )

    waits = jnp.int32(members - 1 + sum(sizes[a] - 1 for a in rest))
    for j in range(1, members):
        greet(place_of(group, lax.rem(me + j, members)))
    for a in rest:
        for j in range(1, sizes[a]):
            greet(place_of((a,), lax.rem(pos[a] + j, sizes[a])))
    for d in DIRS:
        ok = exists(d, 1)
        waits = waits + ok.astype(jnp.int32)

        @pl.when(ok)
        def _(d=d):
            greet(shifted(d, 1))

    def halo_copy(a, i, d, place):
        name, slot = class_slot(d)
        if d[2] == 0:
            src = part(field, (a,), d, edge, False)
        else:
            src = part(zs, (a, 0 if d[2] < 0 else 1), d, edge, False)
        return pltpu.make_async_remote_copy(
            src_ref=src,
            dst_ref=recv[name].at[a, slot],
            send_sem=hs_sem.at[a, i],
            recv_sem=hr_sem.at[a, i],
            device_id=place,
            device_id_type=pl.DeviceIdType.MESH,
        )

    def halo_start(a, values):
        values = values.reshape(cube)
        field[a] = values
        zs[a, 0] = values[:, :, 0:1, :]
        zs[a, 1] = values[:, :, edge:, :]
        for i, d in enumerate(DIRS):

            @pl.when(exists(d, 1))
            def _(i=i, d=d):
                halo_copy(a, i, d, shifted(d, 1)).start()

        field2[a] = values

    def halo_finish(a):
        for i, d in enumerate(DIRS):

            @pl.when(exists(d, -1))
            def _(i=i, d=d):
                halo_copy(a, i, d, shifted(d, -1)).wait_recv()
                name, slot = class_slot(d)
                where = [a]
                for step in d[:2]:
                    where.append(slice(None) if step == 0 else (0 if step > 0 else edge))
                if d[2] != 0:
                    where.append(slice(0, 1) if d[2] > 0 else slice(edge, brick))
                where = tuple(where)
                field2[where] = field2[where] + recv[name][a, slot]

        return field2[a].reshape(count, width)

    def halo_drain(a):
        for i, d in enumerate(DIRS):

            @pl.when(exists(d, 1))
            def _(i=i, d=d):
                halo_copy(a, i, d, shifted(d, 1)).wait_send()

    def rows_at(ref, rank, rows):
        return ref.at[pl.ds(pl.multiple_of(rank * rows, 8), rows)]

    def rs_copy(w, j):
        src, dst = ((ng, rbn), (ea, rba), (eb, rbb))[w]
        to = lax.rem(me + j, members)
        rows = src.shape[0] // members
        return pltpu.make_async_remote_copy(
            src_ref=rows_at(src, to, rows),
            dst_ref=dst.at[j],
            send_sem=rs_s.at[w, j],
            recv_sem=rs_r.at[w, j],
            device_id=place_of(group, to),
            device_id_type=pl.DeviceIdType.MESH,
        )

    def rs_start(w):
        for j in range(1, members):
            rs_copy(w, j).start()

    def rs_finish(w):
        src, dst = ((ng, rbn), (ea, rba), (eb, rbb))[w]
        rows = src.shape[0] // members
        total = rows_at(src, me, rows)[...]
        for j in range(1, members):
            rs_copy(w, j).wait_recv()
            total = total + dst[j]
        return total

    bases = []
    base = 0
    for a in rest:
        bases.append(base)
        base += sizes[a]

    def ex_copy(w, e, j):
        buf = (exn, exa, exb)[w]
        a = rest[e]
        spot = buf.at[bases[e] + pos[a]]
        return pltpu.make_async_remote_copy(
            src_ref=spot,
            dst_ref=spot,
            send_sem=ex_s.at[w, bases[e] + j],
            recv_sem=ex_r.at[w, bases[e] + j],
            device_id=place_of((a,), lax.rem(pos[a] + j, sizes[a])),
            device_id_type=pl.DeviceIdType.MESH,
        )

    def ex_start(w, e, total):
        buf = (exn, exa, exb)[w]
        buf[bases[e] + pos[rest[e]]] = total
        for j in range(1, sizes[rest[e]]):
            ex_copy(w, e, j).start()

    def ex_finish(w, e):
        buf = (exn, exa, exb)[w]
        for j in range(1, sizes[rest[e]]):
            ex_copy(w, e, j).wait_recv()
        total = buf[bases[e]]
        for r in range(1, sizes[rest[e]]):
            total = total + buf[bases[e] + r]
        return total

    def ex_all(w):
        for e in range(len(rest)):
            total = ex_finish(w, e)
            if e + 1 < len(rest):
                ex_start(w, e + 1, total)
        return total

    def ag_copy(w, j):
        buf = (gn, ga, gb)[w]
        spot = rows_at(buf, me, buf.shape[0] // members)
        return pltpu.make_async_remote_copy(
            src_ref=spot,
            dst_ref=spot,
            send_sem=ag_s.at[w, j],
            recv_sem=ag_r.at[w, j],
            device_id=place_of(group, lax.rem(me + j, members)),
            device_id_type=pl.DeviceIdType.MESH,
        )

    def ag_start(w, total):
        buf = (gn, ga, gb)[w]
        rows_at(buf, me, buf.shape[0] // members)[...] = total
        for j in range(1, members):
            ag_copy(w, j).start()

    def ag_finish(w):
        for j in range(1, members):
            ag_copy(w, j).wait_recv()

    node = node_ref[...]
    pad_a[...] = jnp.zeros_like(pad_a)
    pad_s[...] = jnp.zeros_like(pad_s)
    pad_a[1 : brick + 1, 1 : brick + 1] = dot(node, wei[:width]).reshape(cube)
    received = dot(node, wei[width : 2 * width])
    coords = [lax.broadcasted_iota(jnp.int32, cube, axis) for axis in range(3)]
    scale_rows = lax.broadcasted_iota(jnp.int32, (count, brick * brick), 0) // brick
    scale_cols = lax.broadcasted_iota(jnp.int32, (count, brick * brick), 1)
    picked = dot(
        (scale_rows == scale_cols).astype(BF16), cop_ref[...].astype(F32).astype(BF16)
    )
    lane = lax.broadcasted_iota(jnp.int32, (count, brick), 1)
    row = lax.broadcasted_iota(jnp.int32, (count, brick), 0) % brick
    picked = jnp.where(lane == row, picked, 0.0).astype(BF16)
    inverse = 1.0 / dot(picked, jnp.ones((brick, width), BF16))
    fetch.wait()
    hidden_sum = None
    for k in range(kinds):
        o = [offs[k, axis] for axis in range(3)]
        sent = pad_a[pl.ds(1 + o[0], brick), pl.ds(1 + o[1], brick)]
        sent = pltpu.roll(sent.reshape(brick * brick, brick, width), lax.rem(brick - o[2], brick), 1)
        pre = dot(edges[k * count : (k + 1) * count], wei[2 * width :])
        pre = pre + received + sent.reshape(count, width)
        sigma = 0.5 * jnp.tanh(0.5 * pre) + 0.5
        hidden = pre * sigma
        valid = None
        for axis in range(3):
            here = coords[axis] + o[axis]
            one = (here >= 0) & (here < brick)
            valid = one if valid is None else valid & one
        valid = valid.reshape(count, width)
        sl[k] = jnp.where(valid, sigma + hidden * (1.0 - sigma), 0.0)
        hidden = jnp.where(valid, hidden, 0.0).astype(BF16)
        wide = hidden.astype(F32)
        hidden_sum = wide if hidden_sum is None else hidden_sum + wide
    pl.semaphore_wait(barrier, waits)
    halo_start(0, hidden_sum)

    w_out = weo[...]
    cot = cot_ref[...]
    node_own = dot(node, wni[:width])
    upstream = dot_t(cot, wno[...])
    twice = jnp.concatenate([w_out, w_out], axis=0)

    joined = halo_finish(0)
    high = joined.astype(BF16)
    low = (joined - high.astype(F32)).astype(BF16)
    summed = dot(jnp.concatenate([high, low], axis=1), twice)
    gathered = (summed * inverse).astype(BF16)
    pre = node_own + dot(gathered, wni[width:])
    sigma = 0.5 * jnp.tanh(0.5 * pre) + 0.5
    hidden = pre * sigma
    slope = (upstream * (sigma + hidden * (1.0 - sigma))).astype(BF16)
    to_agg = dot_t(slope, wni[width:]) * inverse
    halo_start(1, to_agg)
    ng[:width] = outer(node, slope)
    ng[width : 2 * width] = outer(gathered, slope)
    ng[2 * width : 3 * width] = outer(hidden.astype(BF16), cot)
    ng[3 * width :] = outer(high, to_agg.astype(BF16))
    own = cot.astype(F32) + dot_t(slope, wni[:width])

    arriving = halo_finish(1).astype(BF16)
    rs_start(0)
    back = dot_t(arriving, w_out)
    slopes = []
    direct = None
    turned = None
    for k in range(kinds):
        o = [offs[k, axis] for axis in range(3)]
        slope = (back * sl[k]).astype(BF16)
        slopes.append(slope)
        wide = slope.astype(F32)
        direct = wide if direct is None else direct + wide
        pad_s[k, 1 : brick + 1, 1 : brick + 1] = wide.reshape(cube)
        moved = pad_s[k, pl.ds(1 - o[0], brick), pl.ds(1 - o[1], brick)]
        moved = pltpu.roll(moved.reshape(brick * brick, brick, width), lax.rem(brick + o[2], brick), 1)
        turned = moved if turned is None else turned + moved
    turned = turned.reshape(count, width).astype(BF16)
    direct = direct.astype(BF16)
    slope_all = jnp.concatenate(slopes, axis=0)
    ea[:width] = outer(node, turned)
    ea[width:] = outer(node, direct)
    rs_start(1)
    eb[...] = outer(edges[...], slope_all)
    rs_start(2)
    ex_start(0, 0, rs_finish(0))
    own = own + dot_t(turned, wei[:width]) + dot_t(direct, wei[width : 2 * width])
    halo_start(2, own)
    ex_start(1, 0, rs_finish(1))
    ex_start(2, 0, rs_finish(2))
    ag_start(0, ex_all(0))
    ag_start(1, ex_all(1))
    ag_start(2, ex_all(2))
    egr[...] = dot_t(slope_all, wei[2 * width :]).astype(BF16)
    store = pltpu.make_async_copy(egr, o_edge, out_sem)
    store.start()
    o_node[...] = halo_finish(2).astype(BF16)
    ag_finish(0)
    ag_finish(1)
    ag_finish(2)
    store.wait()
    for a in range(3):
        halo_drain(a)
    for w in range(3):
        for j in range(1, members):
            rs_copy(w, j).wait_send()
            ag_copy(w, j).wait_send()
        for e in range(len(rest)):
            for j in range(1, sizes[rest[e]]):
                ex_copy(w, e, j).wait_send()


def finish(node_in, edge_in, gn, ga, gb, o_node, o_edge, o_ei, o_eo, o_ni, o_no, sems):
    width = gn.shape[1]
    moves = [
        pltpu.make_async_copy(edge_in, o_edge, sems.at[0]),
        pltpu.make_async_copy(node_in, o_node, sems.at[1]),
    ]
    for move in moves:
        move.start()
    totals = [ref[...] for ref in (gn, ga, gb)]
    squares = sum(jnp.sum(t * t, axis=0, keepdims=True) for t in totals)
    squares = jnp.sum(squares, axis=1, keepdims=True)
    entries = sum(t.shape[0] for t in totals) * width
    factor = math.sqrt(entries) / jnp.sqrt(squares)
    o_ei[: 2 * width] = totals[1] * factor
    o_ei[2 * width :] = totals[2] * factor
    o_ni[...] = totals[0][: 2 * width] * factor
    o_no[...] = totals[0][2 * width : 3 * width] * factor
    o_eo[...] = totals[0][3 * width :] * factor
    for move in moves:
        move.wait()


def on_device(
    sizes, node_feat, edge_feat, copies, offsets, w_edge_in, w_edge_out, w_node_in, w_node_out, node_cot
):
    brick = node_feat.shape[0]
    width = node_feat.shape[3]
    kinds = edge_feat.shape[0]
    count = brick**3
    rows_n, rows_a, rows_b = 4 * width, 2 * width, width
    group, rest = ("gx", "gy"), ("gz",)
    if width % (8 * sizes["gx"] * sizes["gy"]) != 0:
        group, rest = ("gy",), ("gx", "gz")
    members = math.prod(sizes[a] for a in group)
    others = sum(sizes[a] for a in rest)
    vmem = pl.BlockSpec(memory_space=pltpu.VMEM)
    smem = pl.BlockSpec(memory_space=pltpu.SMEM)
    hbm = pl.BlockSpec(memory_space=pl.ANY)
    dma = pltpu.SemaphoreType.DMA
    b, w = brick, width
    outs = pl.pallas_call(
        functools.partial(kernel, sizes, group, rest),
        out_shape=(
            jax.ShapeDtypeStruct((count, w), BF16),
            jax.ShapeDtypeStruct((kinds * count, w), BF16),
            jax.ShapeDtypeStruct((rows_n, w), F32),
            jax.ShapeDtypeStruct((rows_a, w), F32),
            jax.ShapeDtypeStruct((rows_b, w), F32),
        ),
        in_specs=[smem, vmem, hbm, vmem, vmem, vmem, vmem, vmem, vmem],
        out_specs=(vmem, hbm, vmem, vmem, vmem),
        scratch_shapes=[
            pltpu.VMEM((kinds * count, w), BF16),
            pltpu.VMEM((kinds * count, w), BF16),
            pltpu.VMEM((b + 2, b + 2, b, w), F32),
            pltpu.VMEM((kinds, b + 2, b + 2, b, w), F32),
            pltpu.VMEM((kinds, count, w), F32),
            pltpu.VMEM((3, b, b, b, w), F32),
            pltpu.VMEM((3, 2, b, b, 1, w), F32),
            pltpu.VMEM((3, b, b, b, w), F32),
            pltpu.VMEM((3, 2, b, b, w), F32),
            pltpu.VMEM((3, 2, b, b, w), F32),
            pltpu.VMEM((3, 2, b, b, 1, w), F32),
            pltpu.VMEM((3, 4, b, w), F32),
            pltpu.VMEM((3, 4, b, 1, w), F32),
            pltpu.VMEM((3, 4, b, 1, w), F32),
            pltpu.VMEM((3, 8, 1, w), F32),
            *[pltpu.VMEM((r, w), F32) for r in (rows_n, rows_a, rows_b)],
            *[pltpu.VMEM((members, r // members, w), F32) for r in (rows_n, rows_a, rows_b)],
            *[pltpu.VMEM((others, r // members, w), F32) for r in (rows_n, rows_a, rows_b)],
            dma,
            dma,
            dma((3, len(DIRS))),
            dma((3, len(DIRS))),
            dma((3, members)),
            dma((3, members)),
            dma((3, others)),
            dma((3, others)),
            dma((3, members)),
            dma((3, members)),
        ],
        compiler_params=pltpu.CompilerParams(
            collective_id=0, has_side_effects=True, vmem_limit_bytes=VMEM_MAIN
        ),
    )(
        offsets,
        node_feat.reshape(count, w),
        edge_feat.reshape(kinds * count, w),
        copies.reshape(b * b, b),
        w_edge_in,
        w_edge_out,
        w_node_in,
        w_node_out,
        node_cot.reshape(count, w),
    )
    done = pl.pallas_call(
        finish,
        out_shape=(
            jax.ShapeDtypeStruct((count, w), BF16),
            jax.ShapeDtypeStruct((kinds * count, w), BF16),
            jax.ShapeDtypeStruct((3 * w, w), F32),
            jax.ShapeDtypeStruct((w, w), F32),
            jax.ShapeDtypeStruct((2 * w, w), F32),
            jax.ShapeDtypeStruct((w, w), F32),
        ),
        in_specs=[FIN, FIN, vmem, vmem, vmem],
        out_specs=(hbm, hbm, vmem, vmem, vmem, vmem),
        scratch_shapes=[dma((2,))],
        compiler_params=pltpu.CompilerParams(vmem_limit_bytes=VMEM_FINISH),
    )(*outs)
    return (done[0].reshape(node_feat.shape), done[1].reshape(edge_feat.shape)) + tuple(done[2:])


def solution(mesh):
    sizes = {a: mesh.shape[a] for a in AXES}
    bricks, edges = P("gx", "gy", "gz", None), P(None, "gx", "gy", "gz", None)
    return jax.shard_map(
        functools.partial(on_device, sizes),
        mesh=mesh,
        in_specs=(bricks, edges, P("gx", "gy", "gz"), P(), P(), P(), P(), P(), bricks),
        out_specs=(bricks, edges, P(), P(), P(), P()),
        check_vma=False,
    )
```

```python
import functools
import math

import jax
import jax.numpy as jnp
from jax import lax
from jax.experimental import pallas as pl
from jax.experimental.pallas import tpu as pltpu
from jax.sharding import PartitionSpec as P

F32 = jnp.float32
BF16 = jnp.bfloat16
VMEM_MAIN = 20 * 2**20
VMEM_FINISH = 8 * 2**20
FIN = pl.BlockSpec(memory_space=pl.ANY)
AXES = ("gx", "gy", "gz")
DIRS = [
    (dx, dy, dz)
    for dx in (-1, 0, 1)
    for dy in (-1, 0, 1)
    for dz in (-1, 0, 1)
    if (dx, dy, dz) != (0, 0, 0)
]


def dot(left, right):
    return jnp.dot(left, right, preferred_element_type=F32)


def dot_t(left, right):
    return lax.dot_general(left, right, (((1,), (1,)), ((), ())), preferred_element_type=F32)


def outer(left, right):
    return lax.dot_general(left, right, (((0,), (0,)), ((), ())), preferred_element_type=F32)


def class_slot(d):
    slot = 0
    for step in d:
        if step != 0:
            slot = slot * 2 + (0 if step < 0 else 1)
    return "".join("xyz"[i] for i in range(3) if d[i] != 0), slot


def part(ref, lead, d, edge, low):
    where = list(lead)
    for step in d[:2]:
        if step == 0:
            where.append(slice(None))
        else:
            where.append(edge if (step > 0) != low else 0)
    return ref.at[tuple(where)]


def kernel(
    sizes, group, rest,
    offs_hbm, node_hbm, edge_hbm, cop_hbm, wei_hbm, weo_hbm, wni_hbm, wno_hbm, cot_hbm,
    o_node, o_edge, gn, ga, gb,
    offs, node_ref, edges, cop_ref, wei, weo, wni, wno, cot_ref, egr, pad_a, pad_s, sl, field, zs, field2,
    rx, ry, rz, rxy, rxz, ryz, rxyz,
    ng, ea, eb, rbn, rba, rbb, exn, exa, exb,
    in_sem, out_sem, hs_sem, hr_sem, rs_s, rs_r, ex_s, ex_r, ag_s, ag_r,
):
    width = node_ref.shape[1]
    count = node_ref.shape[0]
    brick = field.shape[1]
    kinds = offs.shape[0]
    edge = brick - 1
    cube = (brick, brick, brick, width)
    pos = {a: lax.axis_index(a) for a in AXES}
    recv = {"x": rx, "y": ry, "z": rz, "xy": rxy, "xz": rxz, "yz": ryz, "xyz": rxyz}

    fetches = [
        pltpu.make_async_copy(src, dst, in_sem.at[i])
        for i, (src, dst) in enumerate(
            (
                (node_hbm, node_ref), (wei_hbm, wei), (edge_hbm, edges), (cop_hbm, cop_ref),
                (weo_hbm, weo), (wni_hbm, wni), (wno_hbm, wno), (cot_hbm, cot_ref), (offs_hbm, offs),
            )
        )
    ]
    for fetch in fetches:
        fetch.start()

    def exists(d, sign):
        ok = None
        for a, step in zip(AXES, d):
            if step != 0:
                here = pos[a] + sign * step
                one = (here >= 0) & (here < sizes[a])
                ok = one if ok is None else ok & one
        return ok

    def shifted(d, sign):
        return {a: pos[a] + sign * step for a, step in zip(AXES, d)}

    def rank_of(axes):
        rank = 0
        for a in axes:
            rank = rank * sizes[a] + pos[a]
        return rank

    def place_of(axes, rank):
        place = dict(pos)
        for a in reversed(axes):
            place[a] = lax.rem(rank, sizes[a])
            rank = rank // sizes[a]
        return place

    members = math.prod(sizes[a] for a in group)
    me = rank_of(group)

    barrier = pltpu.get_barrier_semaphore()

    def greet(place):
        pl.semaphore_signal(
            barrier, inc=1, device_id=place, device_id_type=pl.DeviceIdType.MESH
        )

    waits = jnp.int32(members - 1 + sum(sizes[a] - 1 for a in rest))
    for j in range(1, members):
        greet(place_of(group, lax.rem(me + j, members)))
    for a in rest:
        for j in range(1, sizes[a]):
            greet(place_of((a,), lax.rem(pos[a] + j, sizes[a])))
    for d in DIRS:
        ok = exists(d, 1)
        waits = waits + ok.astype(jnp.int32)

        @pl.when(ok)
        def _(d=d):
            greet(shifted(d, 1))

    def halo_copy(a, i, d, place):
        name, slot = class_slot(d)
        if d[2] == 0:
            src = part(field, (a,), d, edge, False)
        else:
            src = part(zs, (a, 0 if d[2] < 0 else 1), d, edge, False)
        return pltpu.make_async_remote_copy(
            src_ref=src,
            dst_ref=recv[name].at[a, slot],
            send_sem=hs_sem.at[a, i],
            recv_sem=hr_sem.at[a, i],
            device_id=place,
            device_id_type=pl.DeviceIdType.MESH,
        )

    def halo_start(a, values):
        values = values.reshape(cube)
        field[a] = values
        zs[a, 0] = values[:, :, 0:1, :]
        zs[a, 1] = values[:, :, edge:, :]
        for i, d in enumerate(DIRS):

            @pl.when(exists(d, 1))
            def _(i=i, d=d):
                halo_copy(a, i, d, shifted(d, 1)).start()

        field2[a] = values

    def halo_finish(a):
        for i, d in enumerate(DIRS):

            @pl.when(exists(d, -1))
            def _(i=i, d=d):
                halo_copy(a, i, d, shifted(d, -1)).wait_recv()
                name, slot = class_slot(d)
                where = [a]
                for step in d[:2]:
                    where.append(slice(None) if step == 0 else (0 if step > 0 else edge))
                if d[2] != 0:
                    where.append(slice(0, 1) if d[2] > 0 else slice(edge, brick))
                where = tuple(where)
                field2[where] = field2[where] + recv[name][a, slot]

        return field2[a].reshape(count, width)

    def halo_drain(a):
        for i, d in enumerate(DIRS):

            @pl.when(exists(d, 1))
            def _(i=i, d=d):
                halo_copy(a, i, d, shifted(d, 1)).wait_send()

    def rows_at(ref, rank, rows):
        return ref.at[pl.ds(pl.multiple_of(rank * rows, 8), rows)]

    def rs_copy(w, j):
        src, dst = ((ng, rbn), (ea, rba), (eb, rbb))[w]
        to = lax.rem(me + j, members)
        rows = src.shape[0] // members
        return pltpu.make_async_remote_copy(
            src_ref=rows_at(src, to, rows),
            dst_ref=dst.at[j],
            send_sem=rs_s.at[w, j],
            recv_sem=rs_r.at[w, j],
            device_id=place_of(group, to),
            device_id_type=pl.DeviceIdType.MESH,
        )

    def rs_start(w):
        for j in range(1, members):
            rs_copy(w, j).start()

    def rs_finish(w):
        src, dst = ((ng, rbn), (ea, rba), (eb, rbb))[w]
        rows = src.shape[0] // members
        total = rows_at(src, me, rows)[...]
        for j in range(1, members):
            rs_copy(w, j).wait_recv()
            total = total + dst[j]
        return total

    bases = []
    base = 0
    for a in rest:
        bases.append(base)
        base += sizes[a]

    def ex_copy(w, e, j):
        buf = (exn, exa, exb)[w]
        a = rest[e]
        spot = buf.at[bases[e] + pos[a]]
        return pltpu.make_async_remote_copy(
            src_ref=spot,
            dst_ref=spot,
            send_sem=ex_s.at[w, bases[e] + j],
            recv_sem=ex_r.at[w, bases[e] + j],
            device_id=place_of((a,), lax.rem(pos[a] + j, sizes[a])),
            device_id_type=pl.DeviceIdType.MESH,
        )

    def ex_start(w, e, total):
        buf = (exn, exa, exb)[w]
        buf[bases[e] + pos[rest[e]]] = total
        for j in range(1, sizes[rest[e]]):
            ex_copy(w, e, j).start()

    def ex_finish(w, e):
        buf = (exn, exa, exb)[w]
        for j in range(1, sizes[rest[e]]):
            ex_copy(w, e, j).wait_recv()
        total = buf[bases[e]]
        for r in range(1, sizes[rest[e]]):
            total = total + buf[bases[e] + r]
        return total

    def ex_all(w):
        for e in range(len(rest)):
            total = ex_finish(w, e)
            if e + 1 < len(rest):
                ex_start(w, e + 1, total)
        return total

    def ag_copy(w, j):
        buf = (gn, ga, gb)[w]
        spot = rows_at(buf, me, buf.shape[0] // members)
        return pltpu.make_async_remote_copy(
            src_ref=spot,
            dst_ref=spot,
            send_sem=ag_s.at[w, j],
            recv_sem=ag_r.at[w, j],
            device_id=place_of(group, lax.rem(me + j, members)),
            device_id_type=pl.DeviceIdType.MESH,
        )

    def ag_start(w, total):
        buf = (gn, ga, gb)[w]
        rows_at(buf, me, buf.shape[0] // members)[...] = total
        for j in range(1, members):
            ag_copy(w, j).start()

    def ag_finish(w):
        for j in range(1, members):
            ag_copy(w, j).wait_recv()

    pad_a[...] = jnp.zeros_like(pad_a)
    pad_s[...] = jnp.zeros_like(pad_s)
    for fetch in fetches:
        fetch.wait()
    node = node_ref[...]
    pad_a[1 : brick + 1, 1 : brick + 1] = dot(node, wei[:width]).reshape(cube)
    received = dot(node, wei[width : 2 * width])
    coords = [lax.broadcasted_iota(jnp.int32, cube, axis) for axis in range(3)]
    scale_rows = lax.broadcasted_iota(jnp.int32, (count, brick * brick), 0) // brick
    scale_cols = lax.broadcasted_iota(jnp.int32, (count, brick * brick), 1)
    picked = dot(
        (scale_rows == scale_cols).astype(BF16), cop_ref[...].astype(F32).astype(BF16)
    )
    lane = lax.broadcasted_iota(jnp.int32, (count, brick), 1)
    row = lax.broadcasted_iota(jnp.int32, (count, brick), 0) % brick
    picked = jnp.where(lane == row, picked, 0.0).astype(BF16)
    inverse = 1.0 / dot(picked, jnp.ones((brick, width), BF16))
    hidden_sum = None
    for k in range(kinds):
        o = [offs[k, axis] for axis in range(3)]
        sent = pad_a[pl.ds(1 + o[0], brick), pl.ds(1 + o[1], brick)]
        sent = pltpu.roll(sent.reshape(brick * brick, brick, width), lax.rem(brick - o[2], brick), 1)
        pre = dot(edges[k * count : (k + 1) * count], wei[2 * width :])
        pre = pre + received + sent.reshape(count, width)
        sigma = 0.5 * jnp.tanh(0.5 * pre) + 0.5
        hidden = pre * sigma
        valid = None
        for axis in range(3):
            here = coords[axis] + o[axis]
            one = (here >= 0) & (here < brick)
            valid = one if valid is None else valid & one
        valid = valid.reshape(count, width)
        sl[k] = jnp.where(valid, sigma + hidden * (1.0 - sigma), 0.0)
        hidden = jnp.where(valid, hidden, 0.0).astype(BF16)
        wide = hidden.astype(F32)
        hidden_sum = wide if hidden_sum is None else hidden_sum + wide
    pl.semaphore_wait(barrier, waits)
    halo_start(0, hidden_sum)

    w_out = weo[...]
    cot = cot_ref[...]
    node_own = dot(node, wni[:width])
    upstream = dot_t(cot, wno[...])
    twice = jnp.concatenate([w_out, w_out], axis=0)

    joined = halo_finish(0)
    high = joined.astype(BF16)
    low = (joined - high.astype(F32)).astype(BF16)
    summed = dot(jnp.concatenate([high, low], axis=1), twice)
    gathered = (summed * inverse).astype(BF16)
    pre = node_own + dot(gathered, wni[width:])
    sigma = 0.5 * jnp.tanh(0.5 * pre) + 0.5
    hidden = pre * sigma
    slope = (upstream * (sigma + hidden * (1.0 - sigma))).astype(BF16)
    to_agg = dot_t(slope, wni[width:]) * inverse
    halo_start(1, to_agg)
    ng[:width] = outer(node, slope)
    ng[width : 2 * width] = outer(gathered, slope)
    ng[2 * width : 3 * width] = outer(hidden.astype(BF16), cot)
    ng[3 * width :] = outer(high, to_agg.astype(BF16))
    own = cot.astype(F32) + dot_t(slope, wni[:width])

    arriving = halo_finish(1).astype(BF16)
    rs_start(0)
    back = dot_t(arriving, w_out)
    slopes = []
    direct = None
    turned = None
    for k in range(kinds):
        o = [offs[k, axis] for axis in range(3)]
        slope = (back * sl[k]).astype(BF16)
        slopes.append(slope)
        wide = slope.astype(F32)
        direct = wide if direct is None else direct + wide
        pad_s[k, 1 : brick + 1, 1 : brick + 1] = wide.reshape(cube)
        moved = pad_s[k, pl.ds(1 - o[0], brick), pl.ds(1 - o[1], brick)]
        moved = pltpu.roll(moved.reshape(brick * brick, brick, width), lax.rem(brick + o[2], brick), 1)
        turned = moved if turned is None else turned + moved
    turned = turned.reshape(count, width).astype(BF16)
    direct = direct.astype(BF16)
    slope_all = jnp.concatenate(slopes, axis=0)
    ea[:width] = outer(node, turned)
    ea[width:] = outer(node, direct)
    rs_start(1)
    eb[...] = outer(edges[...], slope_all)
    rs_start(2)
    ex_start(0, 0, rs_finish(0))
    own = own + dot_t(turned, wei[:width]) + dot_t(direct, wei[width : 2 * width])
    halo_start(2, own)
    ex_start(1, 0, rs_finish(1))
    ex_start(2, 0, rs_finish(2))
    ag_start(0, ex_all(0))
    ag_start(1, ex_all(1))
    ag_start(2, ex_all(2))
    egr[...] = dot_t(slope_all, wei[2 * width :]).astype(BF16)
    store = pltpu.make_async_copy(egr, o_edge, out_sem)
    store.start()
    o_node[...] = halo_finish(2).astype(BF16)
    ag_finish(0)
    ag_finish(1)
    ag_finish(2)
    store.wait()
    for a in range(3):
        halo_drain(a)
    for w in range(3):
        for j in range(1, members):
            rs_copy(w, j).wait_send()
            ag_copy(w, j).wait_send()
        for e in range(len(rest)):
            for j in range(1, sizes[rest[e]]):
                ex_copy(w, e, j).wait_send()


def finish(node_in, edge_in, gn, ga, gb, o_node, o_edge, o_ei, o_eo, o_ni, o_no, sems):
    width = gn.shape[1]
    moves = [
        pltpu.make_async_copy(edge_in, o_edge, sems.at[0]),
        pltpu.make_async_copy(node_in, o_node, sems.at[1]),
    ]
    for move in moves:
        move.start()
    totals = [ref[...] for ref in (gn, ga, gb)]
    squares = sum(jnp.sum(t * t, axis=0, keepdims=True) for t in totals)
    squares = jnp.sum(squares, axis=1, keepdims=True)
    entries = sum(t.shape[0] for t in totals) * width
    factor = math.sqrt(entries) / jnp.sqrt(squares)
    o_ei[: 2 * width] = totals[1] * factor
    o_ei[2 * width :] = totals[2] * factor
    o_ni[...] = totals[0][: 2 * width] * factor
    o_no[...] = totals[0][2 * width : 3 * width] * factor
    o_eo[...] = totals[0][3 * width :] * factor
    for move in moves:
        move.wait()


def on_device(
    sizes, node_feat, edge_feat, copies, offsets, w_edge_in, w_edge_out, w_node_in, w_node_out, node_cot
):
    brick = node_feat.shape[0]
    width = node_feat.shape[3]
    kinds = edge_feat.shape[0]
    count = brick**3
    rows_n, rows_a, rows_b = 4 * width, 2 * width, width
    group, rest = ("gx", "gy"), ("gz",)
    if width % (8 * sizes["gx"] * sizes["gy"]) != 0:
        group, rest = ("gy",), ("gx", "gz")
    members = math.prod(sizes[a] for a in group)
    others = sum(sizes[a] for a in rest)
    vmem = pl.BlockSpec(memory_space=pltpu.VMEM)
    hbm = pl.BlockSpec(memory_space=pl.ANY)
    far = pl.BlockSpec(memory_space=pltpu.HBM)
    dma = pltpu.SemaphoreType.DMA
    b, w = brick, width
    outs = pl.pallas_call(
        functools.partial(kernel, sizes, group, rest),
        out_shape=(
            jax.ShapeDtypeStruct((count, w), BF16),
            jax.ShapeDtypeStruct((kinds * count, w), BF16),
            jax.ShapeDtypeStruct((rows_n, w), F32),
            jax.ShapeDtypeStruct((rows_a, w), F32),
            jax.ShapeDtypeStruct((rows_b, w), F32),
        ),
        in_specs=[far] * 9,
        out_specs=(vmem, hbm, vmem, vmem, vmem),
        scratch_shapes=[
            pltpu.SMEM(offsets.shape, jnp.int32),
            pltpu.VMEM((count, w), BF16),
            pltpu.VMEM((kinds * count, w), BF16),
            pltpu.VMEM((b * b, b), jnp.int32),
            pltpu.VMEM((3 * w, w), BF16),
            pltpu.VMEM((w, w), BF16),
            pltpu.VMEM((2 * w, w), BF16),
            pltpu.VMEM((w, w), BF16),
            pltpu.VMEM((count, w), BF16),
            pltpu.VMEM((kinds * count, w), BF16),
            pltpu.VMEM((b + 2, b + 2, b, w), F32),
            pltpu.VMEM((kinds, b + 2, b + 2, b, w), F32),
            pltpu.VMEM((kinds, count, w), F32),
            pltpu.VMEM((3, b, b, b, w), F32),
            pltpu.VMEM((3, 2, b, b, 1, w), F32),
            pltpu.VMEM((3, b, b, b, w), F32),
            pltpu.VMEM((3, 2, b, b, w), F32),
            pltpu.VMEM((3, 2, b, b, w), F32),
            pltpu.VMEM((3, 2, b, b, 1, w), F32),
            pltpu.VMEM((3, 4, b, w), F32),
            pltpu.VMEM((3, 4, b, 1, w), F32),
            pltpu.VMEM((3, 4, b, 1, w), F32),
            pltpu.VMEM((3, 8, 1, w), F32),
            *[pltpu.VMEM((r, w), F32) for r in (rows_n, rows_a, rows_b)],
            *[pltpu.VMEM((members, r // members, w), F32) for r in (rows_n, rows_a, rows_b)],
            *[pltpu.VMEM((others, r // members, w), F32) for r in (rows_n, rows_a, rows_b)],
            dma((9,)),
            dma,
            dma((3, len(DIRS))),
            dma((3, len(DIRS))),
            dma((3, members)),
            dma((3, members)),
            dma((3, others)),
            dma((3, others)),
            dma((3, members)),
            dma((3, members)),
        ],
        compiler_params=pltpu.CompilerParams(
            collective_id=0, has_side_effects=True, vmem_limit_bytes=VMEM_MAIN
        ),
    )(
        pltpu.with_memory_space_constraint(offsets, pltpu.HBM),
        *[
            pltpu.with_memory_space_constraint(array, pltpu.HBM)
            for array in (
                node_feat.reshape(count, w),
                edge_feat.reshape(kinds * count, w),
                copies.reshape(b * b, b),
                w_edge_in,
                w_edge_out,
                w_node_in,
                w_node_out,
                node_cot.reshape(count, w),
            )
        ],
    )
    done = pl.pallas_call(
        finish,
        out_shape=(
            jax.ShapeDtypeStruct((count, w), BF16),
            jax.ShapeDtypeStruct((kinds * count, w), BF16),
            jax.ShapeDtypeStruct((3 * w, w), F32),
            jax.ShapeDtypeStruct((w, w), F32),
            jax.ShapeDtypeStruct((2 * w, w), F32),
            jax.ShapeDtypeStruct((w, w), F32),
        ),
        in_specs=[FIN, FIN, vmem, vmem, vmem],
        out_specs=(hbm, hbm, vmem, vmem, vmem, vmem),
        scratch_shapes=[dma((2,))],
        compiler_params=pltpu.CompilerParams(vmem_limit_bytes=VMEM_FINISH),
    )(*outs)
    return (done[0].reshape(node_feat.shape), done[1].reshape(edge_feat.shape)) + tuple(done[2:])


def solution(mesh):
    sizes = {a: mesh.shape[a] for a in AXES}
    bricks, edges = P("gx", "gy", "gz", None), P(None, "gx", "gy", "gz", None)
    return jax.shard_map(
        functools.partial(on_device, sizes),
        mesh=mesh,
        in_specs=(bricks, edges, P("gx", "gy", "gz"), P(), P(), P(), P(), P(), bricks),
        out_specs=(bricks, edges, P(), P(), P(), P()),
        check_vma=False,
    )
```

```python
import functools
import math

import jax
import jax.numpy as jnp
from jax import lax
from jax.experimental import pallas as pl
from jax.experimental.pallas import tpu as pltpu
from jax.sharding import PartitionSpec as P

F32 = jnp.float32
BF16 = jnp.bfloat16
VMEM_MAIN = 20 * 2**20
VMEM_FINISH = 8 * 2**20
FIN = pl.BlockSpec(memory_space=pl.ANY)
AXES = ("gx", "gy", "gz")
DIRS = [
    (dx, dy, dz)
    for dx in (-1, 0, 1)
    for dy in (-1, 0, 1)
    for dz in (-1, 0, 1)
    if (dx, dy, dz) != (0, 0, 0)
]


def dot(left, right):
    return jnp.dot(left, right, preferred_element_type=F32)


def dot_t(left, right):
    return lax.dot_general(left, right, (((1,), (1,)), ((), ())), preferred_element_type=F32)


def outer(left, right):
    return lax.dot_general(left, right, (((0,), (0,)), ((), ())), preferred_element_type=F32)


def class_slot(d):
    slot = 0
    for step in d:
        if step != 0:
            slot = slot * 2 + (0 if step < 0 else 1)
    return "".join("xyz"[i] for i in range(3) if d[i] != 0), slot


def part(ref, lead, d, edge, low):
    where = list(lead)
    for step in d[:2]:
        if step == 0:
            where.append(slice(None))
        else:
            where.append(edge if (step > 0) != low else 0)
    return ref.at[tuple(where)]


def kernel(
    sizes, group, rest,
    offs_hbm, node_hbm, edge_hbm, cop_hbm, wei_hbm, weo_hbm, wni_hbm, wno_hbm, cot_hbm,
    o_node, o_edge, gn, ga, gb,
    offs, node_ref, edges, cop_ref, wei, weo, wni, wno, cot_ref, egr, pad_a, pad_s, sl, field, zs, field2,
    rx, ry, rz, rxy, rxz, ryz, rxyz,
    ng, ea, eb, rbn, rba, rbb, exn, exa, exb,
    in_sem, out_sem, hs_sem, hr_sem, rs_s, rs_r, ex_s, ex_r, ag_s, ag_r,
):
    width = node_ref.shape[1]
    count = node_ref.shape[0]
    brick = field.shape[1]
    kinds = offs.shape[0]
    edge = brick - 1
    cube = (brick, brick, brick, width)
    pos = {a: lax.axis_index(a) for a in AXES}
    recv = {"x": rx, "y": ry, "z": rz, "xy": rxy, "xz": rxz, "yz": ryz, "xyz": rxyz}

    fetches = [
        pltpu.make_async_copy(src, dst, in_sem.at[i])
        for i, (src, dst) in enumerate(
            (
                (node_hbm, node_ref), (wei_hbm, wei), (edge_hbm, edges), (cop_hbm, cop_ref),
                (weo_hbm, weo), (wni_hbm, wni), (wno_hbm, wno), (cot_hbm, cot_ref), (offs_hbm, offs),
            )
        )
    ]
    for fetch in fetches:
        fetch.start()

    def exists(d, sign):
        ok = None
        for a, step in zip(AXES, d):
            if step != 0:
                here = pos[a] + sign * step
                one = (here >= 0) & (here < sizes[a])
                ok = one if ok is None else ok & one
        return ok

    def shifted(d, sign):
        return {a: pos[a] + sign * step for a, step in zip(AXES, d)}

    def rank_of(axes):
        rank = 0
        for a in axes:
            rank = rank * sizes[a] + pos[a]
        return rank

    def place_of(axes, rank):
        place = dict(pos)
        for a in reversed(axes):
            place[a] = lax.rem(rank, sizes[a])
            rank = rank // sizes[a]
        return place

    members = math.prod(sizes[a] for a in group)
    me = rank_of(group)

    barrier = pltpu.get_barrier_semaphore()

    def greet(place):
        pl.semaphore_signal(
            barrier, inc=1, device_id=place, device_id_type=pl.DeviceIdType.MESH
        )

    waits = jnp.int32(members - 1 + sum(sizes[a] - 1 for a in rest))
    for j in range(1, members):
        greet(place_of(group, lax.rem(me + j, members)))
    for a in rest:
        for j in range(1, sizes[a]):
            greet(place_of((a,), lax.rem(pos[a] + j, sizes[a])))
    for d in DIRS:
        ok = exists(d, 1)
        waits = waits + ok.astype(jnp.int32)

        @pl.when(ok)
        def _(d=d):
            greet(shifted(d, 1))

    def halo_copy(a, i, d, place):
        name, slot = class_slot(d)
        if d[2] == 0:
            src = part(field, (a,), d, edge, False)
        else:
            src = part(zs, (a, 0 if d[2] < 0 else 1), d, edge, False)
        return pltpu.make_async_remote_copy(
            src_ref=src,
            dst_ref=recv[name].at[a, slot],
            send_sem=hs_sem.at[a, i],
            recv_sem=hr_sem.at[a, i],
            device_id=place,
            device_id_type=pl.DeviceIdType.MESH,
        )

    def halo_start(a, values):
        values = values.reshape(cube)
        field[a] = values
        zs[a, 0] = values[:, :, 0:1, :]
        zs[a, 1] = values[:, :, edge:, :]
        for i, d in enumerate(DIRS):

            @pl.when(exists(d, 1))
            def _(i=i, d=d):
                halo_copy(a, i, d, shifted(d, 1)).start()

        field2[a] = values

    def halo_finish(a):
        for i, d in enumerate(DIRS):

            @pl.when(exists(d, -1))
            def _(i=i, d=d):
                halo_copy(a, i, d, shifted(d, -1)).wait_recv()
                name, slot = class_slot(d)
                where = [a]
                for step in d[:2]:
                    where.append(slice(None) if step == 0 else (0 if step > 0 else edge))
                if d[2] != 0:
                    where.append(slice(0, 1) if d[2] > 0 else slice(edge, brick))
                where = tuple(where)
                field2[where] = field2[where] + recv[name][a, slot]

        return field2[a].reshape(count, width)

    def halo_drain(a):
        for i, d in enumerate(DIRS):

            @pl.when(exists(d, 1))
            def _(i=i, d=d):
                halo_copy(a, i, d, shifted(d, 1)).wait_send()

    def rows_at(ref, rank, rows):
        return ref.at[pl.ds(pl.multiple_of(rank * rows, 8), rows)]

    def rs_copy(w, j):
        src, dst = ((ng, rbn), (ea, rba), (eb, rbb))[w]
        to = lax.rem(me + j, members)
        rows = src.shape[0] // members
        return pltpu.make_async_remote_copy(
            src_ref=rows_at(src, to, rows),
            dst_ref=dst.at[j],
            send_sem=rs_s.at[w, j],
            recv_sem=rs_r.at[w, j],
            device_id=place_of(group, to),
            device_id_type=pl.DeviceIdType.MESH,
        )

    def rs_start(w):
        for j in range(1, members):
            rs_copy(w, j).start()

    def rs_finish(w):
        src, dst = ((ng, rbn), (ea, rba), (eb, rbb))[w]
        rows = src.shape[0] // members
        total = rows_at(src, me, rows)[...]
        for j in range(1, members):
            rs_copy(w, j).wait_recv()
            total = total + dst[j]
        return total

    bases = []
    base = 0
    for a in rest:
        bases.append(base)
        base += sizes[a]

    def ex_copy(w, e, j):
        buf = (exn, exa, exb)[w]
        a = rest[e]
        spot = buf.at[bases[e] + pos[a]]
        return pltpu.make_async_remote_copy(
            src_ref=spot,
            dst_ref=spot,
            send_sem=ex_s.at[w, bases[e] + j],
            recv_sem=ex_r.at[w, bases[e] + j],
            device_id=place_of((a,), lax.rem(pos[a] + j, sizes[a])),
            device_id_type=pl.DeviceIdType.MESH,
        )

    def ex_start(w, e, total):
        buf = (exn, exa, exb)[w]
        buf[bases[e] + pos[rest[e]]] = total
        for j in range(1, sizes[rest[e]]):
            ex_copy(w, e, j).start()

    def ex_finish(w, e):
        buf = (exn, exa, exb)[w]
        for j in range(1, sizes[rest[e]]):
            ex_copy(w, e, j).wait_recv()
        total = buf[bases[e]]
        for r in range(1, sizes[rest[e]]):
            total = total + buf[bases[e] + r]
        return total

    def ex_all(w):
        for e in range(len(rest)):
            total = ex_finish(w, e)
            if e + 1 < len(rest):
                ex_start(w, e + 1, total)
        return total

    def ag_copy(w, j):
        buf = (gn, ga, gb)[w]
        spot = rows_at(buf, me, buf.shape[0] // members)
        return pltpu.make_async_remote_copy(
            src_ref=spot,
            dst_ref=spot,
            send_sem=ag_s.at[w, j],
            recv_sem=ag_r.at[w, j],
            device_id=place_of(group, lax.rem(me + j, members)),
            device_id_type=pl.DeviceIdType.MESH,
        )

    def ag_start(w, total):
        buf = (gn, ga, gb)[w]
        rows_at(buf, me, buf.shape[0] // members)[...] = total
        for j in range(1, members):
            ag_copy(w, j).start()

    def ag_finish(w):
        for j in range(1, members):
            ag_copy(w, j).wait_recv()

    pad_a[...] = jnp.zeros_like(pad_a)
    pad_s[...] = jnp.zeros_like(pad_s)
    for fetch in fetches:
        fetch.wait()
    node = node_ref[...]
    pad_a[1 : brick + 1, 1 : brick + 1] = dot(node, wei[:width]).reshape(cube)
    received = dot(node, wei[width : 2 * width])
    coords = [lax.broadcasted_iota(jnp.int32, cube, axis) for axis in range(3)]
    scale_rows = lax.broadcasted_iota(jnp.int32, (count, brick * brick), 0) // brick
    scale_cols = lax.broadcasted_iota(jnp.int32, (count, brick * brick), 1)
    picked = dot(
        (scale_rows == scale_cols).astype(BF16), cop_ref[...].astype(F32).astype(BF16)
    )
    lane = lax.broadcasted_iota(jnp.int32, (count, brick), 1)
    row = lax.broadcasted_iota(jnp.int32, (count, brick), 0) % brick
    picked = jnp.where(lane == row, picked, 0.0).astype(BF16)
    inverse = 1.0 / dot(picked, jnp.ones((brick, width), BF16))
    hidden_sum = None
    for k in range(kinds):
        o = [offs[k, axis] for axis in range(3)]
        sent = pad_a[pl.ds(1 + o[0], brick), pl.ds(1 + o[1], brick)]
        sent = pltpu.roll(sent.reshape(brick * brick, brick, width), lax.rem(brick - o[2], brick), 1)
        pre = dot(edges[k * count : (k + 1) * count], wei[2 * width :])
        pre = pre + received + sent.reshape(count, width)
        sigma = 0.5 * jnp.tanh(0.5 * pre) + 0.5
        hidden = pre * sigma
        valid = None
        for axis in range(3):
            here = coords[axis] + o[axis]
            one = (here >= 0) & (here < brick)
            valid = one if valid is None else valid & one
        valid = valid.reshape(count, width)
        sl[k] = jnp.where(valid, sigma + hidden * (1.0 - sigma), 0.0)
        hidden = jnp.where(valid, hidden, 0.0).astype(BF16)
        wide = hidden.astype(F32)
        hidden_sum = wide if hidden_sum is None else hidden_sum + wide
    pl.semaphore_wait(barrier, waits)
    halo_start(0, hidden_sum)

    w_out = weo[...]
    cot = cot_ref[...]
    node_own = dot(node, wni[:width])
    upstream = dot_t(cot, wno[...])
    twice = jnp.concatenate([w_out, w_out], axis=0)

    joined = halo_finish(0)
    high = joined.astype(BF16)
    low = (joined - high.astype(F32)).astype(BF16)
    summed = dot(jnp.concatenate([high, low], axis=1), twice)
    gathered = (summed * inverse).astype(BF16)
    pre = node_own + dot(gathered, wni[width:])
    sigma = 0.5 * jnp.tanh(0.5 * pre) + 0.5
    hidden = pre * sigma
    slope = (upstream * (sigma + hidden * (1.0 - sigma))).astype(BF16)
    to_agg = dot_t(slope, wni[width:]) * inverse
    halo_start(1, to_agg)
    ng[:width] = outer(node, slope)
    ng[width : 2 * width] = outer(gathered, slope)
    ng[2 * width : 3 * width] = outer(hidden.astype(BF16), cot)
    ng[3 * width :] = outer(high, to_agg.astype(BF16))
    rs_start(0)
    own = cot.astype(F32) + dot_t(slope, wni[:width])

    arriving = halo_finish(1).astype(BF16)
    back = dot_t(arriving, w_out)
    slopes = []
    direct = None
    turned = None
    for k in range(kinds):
        o = [offs[k, axis] for axis in range(3)]
        slope = (back * sl[k]).astype(BF16)
        slopes.append(slope)
        wide = slope.astype(F32)
        direct = wide if direct is None else direct + wide
        pad_s[k, 1 : brick + 1, 1 : brick + 1] = wide.reshape(cube)
        moved = pad_s[k, pl.ds(1 - o[0], brick), pl.ds(1 - o[1], brick)]
        moved = pltpu.roll(moved.reshape(brick * brick, brick, width), lax.rem(brick + o[2], brick), 1)
        turned = moved if turned is None else turned + moved
    turned = turned.reshape(count, width).astype(BF16)
    direct = direct.astype(BF16)
    slope_all = jnp.concatenate(slopes, axis=0)
    ea[:width] = outer(node, turned)
    ea[width:] = outer(node, direct)
    rs_start(1)
    eb[...] = outer(edges[...], slope_all)
    rs_start(2)
    ex_start(0, 0, rs_finish(0))
    own = own + dot_t(turned, wei[:width]) + dot_t(direct, wei[width : 2 * width])
    ex_start(1, 0, rs_finish(1))
    ex_start(2, 0, rs_finish(2))
    halo_start(2, own)
    ag_start(0, ex_all(0))
    ag_start(1, ex_all(1))
    ag_start(2, ex_all(2))
    egr[...] = dot_t(slope_all, wei[2 * width :]).astype(BF16)
    store = pltpu.make_async_copy(egr, o_edge, out_sem)
    store.start()
    o_node[...] = halo_finish(2).astype(BF16)
    ag_finish(0)
    ag_finish(1)
    ag_finish(2)
    store.wait()
    for a in range(3):
        halo_drain(a)
    for w in range(3):
        for j in range(1, members):
            rs_copy(w, j).wait_send()
            ag_copy(w, j).wait_send()
        for e in range(len(rest)):
            for j in range(1, sizes[rest[e]]):
                ex_copy(w, e, j).wait_send()


def finish(node_in, edge_in, gn, ga, gb, o_node, o_edge, o_ei, o_eo, o_ni, o_no, sems):
    width = gn.shape[1]
    moves = [
        pltpu.make_async_copy(edge_in, o_edge, sems.at[0]),
        pltpu.make_async_copy(node_in, o_node, sems.at[1]),
    ]
    for move in moves:
        move.start()
    totals = [ref[...] for ref in (gn, ga, gb)]
    squares = sum(jnp.sum(t * t, axis=0, keepdims=True) for t in totals)
    squares = jnp.sum(squares, axis=1, keepdims=True)
    entries = sum(t.shape[0] for t in totals) * width
    factor = math.sqrt(entries) / jnp.sqrt(squares)
    o_ei[: 2 * width] = totals[1] * factor
    o_ei[2 * width :] = totals[2] * factor
    o_ni[...] = totals[0][: 2 * width] * factor
    o_no[...] = totals[0][2 * width : 3 * width] * factor
    o_eo[...] = totals[0][3 * width :] * factor
    for move in moves:
        move.wait()


def on_device(
    sizes, node_feat, edge_feat, copies, offsets, w_edge_in, w_edge_out, w_node_in, w_node_out, node_cot
):
    brick = node_feat.shape[0]
    width = node_feat.shape[3]
    kinds = edge_feat.shape[0]
    count = brick**3
    rows_n, rows_a, rows_b = 4 * width, 2 * width, width
    group, rest = ("gx", "gy"), ("gz",)
    if width % (8 * sizes["gx"] * sizes["gy"]) != 0:
        group, rest = ("gy",), ("gx", "gz")
    members = math.prod(sizes[a] for a in group)
    others = sum(sizes[a] for a in rest)
    vmem = pl.BlockSpec(memory_space=pltpu.VMEM)
    hbm = pl.BlockSpec(memory_space=pl.ANY)
    far = pl.BlockSpec(memory_space=pltpu.HBM)
    dma = pltpu.SemaphoreType.DMA
    b, w = brick, width
    outs = pl.pallas_call(
        functools.partial(kernel, sizes, group, rest),
        out_shape=(
            jax.ShapeDtypeStruct((count, w), BF16),
            jax.ShapeDtypeStruct((kinds * count, w), BF16),
            jax.ShapeDtypeStruct((rows_n, w), F32),
            jax.ShapeDtypeStruct((rows_a, w), F32),
            jax.ShapeDtypeStruct((rows_b, w), F32),
        ),
        in_specs=[far] * 9,
        out_specs=(vmem, hbm, vmem, vmem, vmem),
        scratch_shapes=[
            pltpu.SMEM(offsets.shape, jnp.int32),
            pltpu.VMEM((count, w), BF16),
            pltpu.VMEM((kinds * count, w), BF16),
            pltpu.VMEM((b * b, b), jnp.int32),
            pltpu.VMEM((3 * w, w), BF16),
            pltpu.VMEM((w, w), BF16),
            pltpu.VMEM((2 * w, w), BF16),
            pltpu.VMEM((w, w), BF16),
            pltpu.VMEM((count, w), BF16),
            pltpu.VMEM((kinds * count, w), BF16),
            pltpu.VMEM((b + 2, b + 2, b, w), F32),
            pltpu.VMEM((kinds, b + 2, b + 2, b, w), F32),
            pltpu.VMEM((kinds, count, w), F32),
            pltpu.VMEM((3, b, b, b, w), F32),
            pltpu.VMEM((3, 2, b, b, 1, w), F32),
            pltpu.VMEM((3, b, b, b, w), F32),
            pltpu.VMEM((3, 2, b, b, w), F32),
            pltpu.VMEM((3, 2, b, b, w), F32),
            pltpu.VMEM((3, 2, b, b, 1, w), F32),
            pltpu.VMEM((3, 4, b, w), F32),
            pltpu.VMEM((3, 4, b, 1, w), F32),
            pltpu.VMEM((3, 4, b, 1, w), F32),
            pltpu.VMEM((3, 8, 1, w), F32),
            *[pltpu.VMEM((r, w), F32) for r in (rows_n, rows_a, rows_b)],
            *[pltpu.VMEM((members, r // members, w), F32) for r in (rows_n, rows_a, rows_b)],
            *[pltpu.VMEM((others, r // members, w), F32) for r in (rows_n, rows_a, rows_b)],
            dma((9,)),
            dma,
            dma((3, len(DIRS))),
            dma((3, len(DIRS))),
            dma((3, members)),
            dma((3, members)),
            dma((3, others)),
            dma((3, others)),
            dma((3, members)),
            dma((3, members)),
        ],
        compiler_params=pltpu.CompilerParams(
            collective_id=0, has_side_effects=True, vmem_limit_bytes=VMEM_MAIN
        ),
    )(
        pltpu.with_memory_space_constraint(offsets, pltpu.HBM),
        *[
            pltpu.with_memory_space_constraint(array, pltpu.HBM)
            for array in (
                node_feat.reshape(count, w),
                edge_feat.reshape(kinds * count, w),
                copies.reshape(b * b, b),
                w_edge_in,
                w_edge_out,
                w_node_in,
                w_node_out,
                node_cot.reshape(count, w),
            )
        ],
    )
    done = pl.pallas_call(
        finish,
        out_shape=(
            jax.ShapeDtypeStruct((count, w), BF16),
            jax.ShapeDtypeStruct((kinds * count, w), BF16),
            jax.ShapeDtypeStruct((3 * w, w), F32),
            jax.ShapeDtypeStruct((w, w), F32),
            jax.ShapeDtypeStruct((2 * w, w), F32),
            jax.ShapeDtypeStruct((w, w), F32),
        ),
        in_specs=[FIN, FIN, vmem, vmem, vmem],
        out_specs=(hbm, hbm, vmem, vmem, vmem, vmem),
        scratch_shapes=[dma((2,))],
        compiler_params=pltpu.CompilerParams(vmem_limit_bytes=VMEM_FINISH),
    )(*outs)
    return (done[0].reshape(node_feat.shape), done[1].reshape(edge_feat.shape)) + tuple(done[2:])


def solution(mesh):
    sizes = {a: mesh.shape[a] for a in AXES}
    bricks, edges = P("gx", "gy", "gz", None), P(None, "gx", "gy", "gz", None)
    return jax.shard_map(
        functools.partial(on_device, sizes),
        mesh=mesh,
        in_specs=(bricks, edges, P("gx", "gy", "gz"), P(), P(), P(), P(), P(), bricks),
        out_specs=(bricks, edges, P(), P(), P(), P()),
        check_vma=False,
    )
```
